512 devices in a mesh: section: 16 (over x_hi, z), expert: 32 (over x_lo, y, core).
Axes of the slice: x: 4 (x_hi: 2, x_lo: 2; x = x_hi * 2 + x_lo), y: 8, z: 8, core: 2. Of those that a mesh axis runs over, the one named last changes fastest.
Arguments:
- tokens: bfloat16 [4096, 6144], P('expert', 'section'), may hold values from -12 to 12
- route: int32 [4096, 2], P('expert'), may hold values from 0 to 7, all different within a row; in each aligned block of 128 rows (0 to 127, 128 to 255, ...) at most 40 rows name the same one
- norm_gain: float32 [6144], replicated, may hold values from 0.5 to 1.5
- router: bfloat16 [6144, 8], replicated, may hold values from -0.078125 to 0.078125
- gate_weight: bfloat16 [32, 16, 128, 6144], P('expert', 'section'), may hold values from -0.078125 to 0.078125
- up_weight: bfloat16 [32, 16, 128, 6144], P('expert', 'section'), may hold values from -0.078125 to 0.078125
Outputs:
- expert_hidden: bfloat16 [32, 32, 40, 16, 128], P('expert', None, None, 'section')
The draws below stay inside these ranges and needn't reach their ends.
Inputs may be any that keep to these rules, and one draw needn't show every extreme that they name: `route`: among the 128 tokens of one index of expert no expert is named more than 40 times, and a token's two ids differ.
All inputs are finite; a program needn't handle non-finite values.
Results may differ from the reference program's by a relative error of at most 0.0065.
Values may be sent and summed in bfloat16 or wider, within the bound.
A program may use at most 64 MiB of HBM per device.

```python
import math
import jax
import jax.numpy as jnp
import numpy as np
from jax import lax

D = 6144
EXPERTS = 8
TOP = 2
TOK_DEV = 128
CAPACITY = 40
SECTIONS = 16
SLOTS = 32
GROUP = 4
FF_DEV = 128
TOKENS = 4096


def draw_tokens(key, part):
    column = jnp.arange(D, dtype=jnp.float32) / (D - 1)
    base = jax.random.normal(key, (TOKENS, D), jnp.float32)
    return jnp.clip(0.6 * base * jnp.exp(column * math.log(3.0)), -12.0, 12.0).astype(jnp.bfloat16)


def block_levels(key, shape, shards, low, high):
    loudness, own = 1.0, jax.random.fold_in(key, 6)
    for dim, shards_of in shards:
        steps = jnp.exp(jax.random.uniform(jax.random.fold_in(own, dim), (shards_of,), jnp.float32, low / len(shards), high / len(shards)))
        loudness = loudness * jnp.repeat(steps, shape[dim] // shards_of).reshape([-1 if axis == dim else 1 for axis in range(len(shape))])
    return loudness


def routed_block(key, own, number, rows, count, top, limit, lean):
    ranking = jax.random.permutation(key, count)
    packed, usual = load_shares(count, rows * top, limit, lean, True), load_shares(count, rows * top, limit, lean, False)
    places = jnp.arange(count)

    def named(tallies, offset_by):
        used = int((tallies > 0).sum())
        fixed = max(1, used // 4)
        passed = fixed + (places - fixed + offset_by * (used - fixed)) % max(1, count - fixed)
        return jnp.zeros((count,), jnp.int32).at[ranking[jnp.where(places < fixed, places, passed)]].set(jnp.asarray(tallies, jnp.int32))

    tallies = jnp.where(number % 4 == 0, named(packed, number // 4), named(usual, number - number // 4 - 1))
    mixed = jax.random.permutation(jax.random.fold_in(own, 3), count)
    giver, taker = mixed[0:count // 2 * 2:2], mixed[1:count // 2 * 2:2]
    slack = jnp.minimum(tallies[giver] - 1, limit - tallies[taker]) // 2
    slack = jnp.where((giver == ranking[0]) | (taker == ranking[0]) | (tallies[taker] == 0), 0, jnp.maximum(slack, 0))
    passed = jax.random.randint(jax.random.fold_in(own, 4), (count // 2,), 0, 1 << 20) % (slack + 1)
    tallies = tallies.at[giver].add(-passed).at[taker].add(passed)
    labels = jnp.searchsorted(jnp.cumsum(tallies), jnp.arange(rows * top), side="right").astype(jnp.int32)
    table = labels.reshape(top, rows).T
    table = table[jax.random.permutation(jax.random.fold_in(own, 1), rows)]
    offset_by = jax.random.randint(jax.random.fold_in(own, 2), (rows, 1), 0, top)
    return jnp.take_along_axis(table, (jnp.arange(top)[None, :] + offset_by) % top, axis=1)


def load_shares(count, total, bound, skew, full):
    portions = [(1 << 20) // math.isqrt(standing ** skew) + 1 for standing in range(1, count + 1)]
    largest = bound if full else min(bound, max(-(-total // count), total * portions[0] // sum(portions)))
    least = 1 if total - largest >= count - 1 else 0
    given, surplus = [largest] + [least] * (count - 1), total - largest - least * (count - 1)
    while surplus > 0:
        movable = [i for i in range(1, count) if given[i] < largest] or [i for i in range(1, count) if given[i] < bound]
        whole, left = sum([portions[i] for i in movable]), surplus
        for i in movable:
            extra = min(bound - given[i], max(1, left * portions[i] // whole), surplus)
            given[i] = given[i] + extra
            surplus = surplus - extra
    return np.array(given)


def scatter_about(key, dims, scale, limit, split=(), kind=jnp.bfloat16):
    result = jax.random.normal(key, dims, jnp.float32) * scale
    if len(split) > 0:
        result = block_levels(key, dims, split, -0.22, 0.18) * result
    return jnp.clip(result, min=-limit, max=limit).astype(kind)


def setup_inputs(seed: int = 0) -> dict:
    key_of = jax.random.split(jax.random.key(seed), 7)
    tokens = draw_tokens(jax.random.fold_in(key_of[6], 71), 0)
    route_keys = jax.random.split(jax.random.fold_in(key_of[1], 1), TOKENS // TOK_DEV)
    route_turns = jax.random.permutation(jax.random.fold_in(key_of[1], 3), TOKENS // TOK_DEV)
    route = jax.vmap(lambda own, number: routed_block(jax.random.fold_in(key_of[1], 2), own, number, TOK_DEV, EXPERTS, 2, CAPACITY, 0))(route_keys, route_turns).reshape((TOKENS, TOP))
    norm_gain = jnp.clip(1.0 + 0.1 * jax.random.normal(key_of[2], (D,), jnp.float32), 0.5, 1.5)
    router = scatter_about(key_of[3], (D, EXPERTS), D ** -0.5, 0.078125)
    gate_weight = scatter_about(key_of[4], (SLOTS, SECTIONS, FF_DEV, D), D ** -0.5, 0.078125, ((0, 32), (1, 16)))
    up_weight = scatter_about(key_of[5], (SLOTS, SECTIONS, FF_DEV, D), D ** -0.5, 0.078125, ((0, 32), (1, 16)))
    return dict(tokens=tokens, route=route, norm_gain=norm_gain, router=router, gate_weight=gate_weight, up_weight=up_weight)


def reference(tokens, route, norm_gain, router, gate_weight, up_weight):
    as_float = tokens.astype(jnp.float32)
    mean_square = lax.optimization_barrier(jnp.mean(as_float * as_float, axis=-1, keepdims=True))
    normed = (as_float * lax.rsqrt(mean_square + 1e-05) * norm_gain).astype(jnp.bfloat16)
    logits = jnp.dot(normed, router, preferred_element_type=jnp.float32)
    one_hot = route[:, :, None] == jnp.arange(EXPERTS, dtype=jnp.int32)[None, None, :]
    picked = lax.optimization_barrier(jnp.sum(jnp.where(one_hot, logits[:, None, :], jnp.float32(0.0)), axis=-1))
    weight_first = 1.0 / (1.0 + jnp.exp(picked[:, 1] - picked[:, 0]))
    weight_second = 1.0 / (1.0 + jnp.exp(picked[:, 0] - picked[:, 1]))
    weight_pair = jnp.stack([weight_first, weight_second], axis=1).astype(jnp.bfloat16)
    flat_hot = one_hot.reshape(SLOTS, 2 * TOK_DEV, EXPERTS).astype(jnp.int32)
    slot_rank = lax.optimization_barrier(jnp.sum((jnp.cumsum(flat_hot, axis=1) - flat_hot) * flat_hot, axis=-1))
    rank_hot = slot_rank[:, :, None] == jnp.arange(CAPACITY, dtype=jnp.int32)[None, None, :]
    placing = ((flat_hot[:, :, :, None] > 0) & rank_hot[:, :, None, :]).astype(jnp.float32)
    doubled = jnp.repeat(normed.reshape(SLOTS, TOK_DEV, D), 2, axis=1).astype(jnp.float32)
    rows = jnp.einsum('drec,drk->edck', placing, doubled).astype(jnp.bfloat16)
    pair_flat = weight_pair.reshape(SLOTS, 2 * TOK_DEV).astype(jnp.float32)
    row_weight = jnp.einsum('drec,dr->edc', placing, pair_flat)

    def one_slot(slot_index):
        expert_index = (slot_index // GROUP).astype(jnp.int32)
        expert_rows = lax.dynamic_index_in_dim(rows, expert_index, 0, keepdims=False).reshape(SLOTS * CAPACITY, D)
        expert_weight = lax.dynamic_index_in_dim(row_weight, expert_index, 0, keepdims=False).reshape(SLOTS * CAPACITY, 1)
        gate_block = lax.dynamic_index_in_dim(gate_weight, slot_index, 0, keepdims=False).reshape(SECTIONS * FF_DEV, D)
        up_block = lax.dynamic_index_in_dim(up_weight, slot_index, 0, keepdims=False).reshape(SECTIONS * FF_DEV, D)
        gate = jnp.dot(expert_rows, gate_block.T, preferred_element_type=jnp.float32)
        upper = jnp.dot(expert_rows, up_block.T, preferred_element_type=jnp.float32)
        hidden = (jax.nn.silu(gate) * upper * expert_weight).astype(jnp.bfloat16)
        return hidden.reshape(SLOTS, CAPACITY, SECTIONS, FF_DEV)
    return lax.map(one_slot, jnp.arange(SLOTS, dtype=jnp.int32))
```

```python
import jax
import jax.numpy as jnp
from jax import lax
from jax.experimental import pallas as pl
from jax.experimental.pallas import tpu as pltpu
from jax.sharding import PartitionSpec as P

D = 6144
Z = 8
ROWS = 640
WIDTH = 384
EARLY = 448
COPIES = 80


def gather_matmul(own_ref, stat_ref, gate_ref, up_ref, acc_ref, tot_ref, full, stats, send, recv, local):
    sec = lax.axis_index("section")
    exp = lax.axis_index("expert")
    plane, z = sec // Z, lax.rem(sec, Z)
    core = lax.rem(exp, 2)
    up_sec = plane * Z + lax.rem(z + 1, Z)
    down_sec = plane * Z + lax.rem(z + Z - 1, Z)
    across_sec = (1 - plane) * Z + z
    peers = dict(
        up=(up_sec, exp),
        down=(down_sec, exp),
        across=(across_sec, exp),
        partner=(sec, exp + 1 - 2 * core),
    )
    barrier = pltpu.get_barrier_semaphore()
    for peer in peers.values():
        pl.semaphore_signal(barrier, inc=1, device_id=peer, device_id_type=pl.DeviceIdType.MESH)
    pl.semaphore_wait(barrier, len(peers))

    shift = (0, Z - 1, Z - 2, Z - 3, 1, 2, 3, 4)

    def mine(i):
        return plane * Z + lax.rem(z + shift[i], Z)

    def other(i):
        return (1 - plane) * Z + lax.rem(z + shift[i], Z)

    made = {}

    def start(name, peer, src, dst):
        n = len(made)
        copy = pltpu.make_async_remote_copy(
            src_ref=src,
            dst_ref=dst,
            send_sem=send.at[n],
            recv_sem=recv.at[n],
            device_id=peers[peer],
            device_id_type=pl.DeviceIdType.MESH,
        )
        copy.start()
        made[name] = copy

    def rows(i_sec, lo, n):
        return full.at[i_sec, core, pl.ds(lo, n)]

    early, late = (0, EARLY), (EARLY, ROWS - EARLY)

    def ring(kind, i, way, hop):
        n = ROWS if kind == 0 else EARLY
        lo = 0
        if hop == 4:
            n = n // 2
            lo = 0 if way == "up" else n
        dst = rows(mine(i) if kind == 0 else other(i), lo, n)
        src = own_ref.at[pl.ds(lo, n)] if (kind == 0 and i == 0) else dst
        start(("ring", kind, way, hop), way, src, dst)

    def ring_stat(i, way, hop):
        dst = stats.at[mine(i), core]
        start(("stat", way, hop), way, stat_ref if i == 0 else dst, dst)

    def spread(i):
        dst = rows(mine(i), *late)
        start(("late", i), "across", own_ref.at[pl.ds(*late)] if i == 0 else dst, dst)
        dst = stats.at[mine(i), core]
        src = stat_ref if i == 0 else dst
        start(("sx", i), "across", src, dst)
        start(("ps", i), "partner", src, dst)
        dst = rows(mine(i), 0, ROWS)
        start(("p0", i), "partner", own_ref if i == 0 else dst, dst)

    def spread_early(i):
        dst = rows(other(i), *early)
        start(("pe", i), "partner", dst, dst)

    def spread_late(i):
        made[("late", i)].wait_recv()
        made[("sx", i)].wait_recv()
        dst = rows(other(i), *late)
        start(("pl", i), "partner", dst, dst)
        dst = stats.at[other(i), core]
        start(("po", i), "partner", dst, dst)

    def multiply(s, first):
        cols = pl.ds(pl.multiple_of(s * WIDTH, 128), WIDTH)
        weights = jnp.concatenate([gate_ref[:, cols], up_ref[:, cols]], axis=0)

        @pl.loop(0, 4)
        def _(t):
            at = pl.ds(pl.multiple_of(lax.rem(t, 2) * 320, 32), 320)
            to = pl.ds(pl.multiple_of(t * 320, 32), 320)
            part = lax.dot_general(
                full[s, t // 2, at, :], weights, (((1,), (1,)), ((), ())),
                preferred_element_type=jnp.float32,
            )
            if first:
                acc_ref[to, :] = part
            else:
                acc_ref[to, :] += part

    def consume(i):
        made[("p0", i)].wait_recv()
        multiply(mine(i), i == 0)
        made[("pe", i)].wait_recv()
        made[("pl", i)].wait_recv()
        multiply(other(i), False)

    dst = rows(other(0), *early)
    start(("early",), "across", own_ref.at[pl.ds(*early)], rows(sec, *early))
    ring(0, 0, "up", 1)
    ring(0, 0, "down", 1)
    ring_stat(0, "up", 1)
    ring_stat(0, "down", 1)
    spread(0)
    keep = pltpu.make_async_copy(own_ref, full.at[sec, core], local.at[0])
    keep.start()
    keep_stat = pltpu.make_async_copy(stat_ref, stats.at[sec, core], local.at[1])
    keep_stat.start()
    made[("early",)].wait_recv()
    ring(1, 0, "up", 1)
    ring(1, 0, "down", 1)
    spread_early(0)
    keep.wait()
    keep_stat.wait()
    ways = (("up", 0), ("down", 3))
    for hop in (1, 2, 3):
        for way, base in ways:
            made[("ring", 0, way, hop)].wait_recv()
            ring(0, base + hop, way, hop + 1)
            made[("stat", way, hop)].wait_recv()
            if hop < 3 or way == "up":
                ring_stat(base + hop, way, hop + 1)
            spread(base + hop)
        for way, base in ways:
            made[("ring", 1, way, hop)].wait_recv()
            ring(1, base + hop, way, hop + 1)
            spread_early(base + hop)
        before = [0] if hop == 1 else [hop - 1, hop + 2]
        for i in before:
            spread_late(i)
        for i in before:
            consume(i)
    for way, _ in ways:
        made[("ring", 0, way, 4)].wait_recv()
    made[("stat", "up", 4)].wait_recv()
    spread(7)
    for way, _ in ways:
        made[("ring", 1, way, 4)].wait_recv()
    spread_early(7)
    for i in (3, 6):
        spread_late(i)
    for i in (3, 6):
        consume(i)
    spread_late(7)
    consume(7)
    for i in range(8):
        made[("ps", i)].wait_recv()
        made[("po", i)].wait_recv()
    tot_ref[...] = jnp.sum(stats[...], axis=0)
    for copy in made.values():
        copy.wait_send()


def place_rows(scaled, square_part, logit_part, route, expert_count, capacity):
    one_hot = route[:, :, None] == jnp.arange(expert_count, dtype=jnp.int32)[None, None, :]
    picked = jnp.sum(jnp.where(one_hot, logit_part[:, None, :], jnp.float32(0.0)), axis=-1)
    lead = jnp.stack([picked[:, 1] - picked[:, 0], picked[:, 0] - picked[:, 1]], axis=1).reshape(-1)
    square = jnp.repeat(square_part, 2)
    flat_hot = one_hot.reshape(-1, expert_count).astype(jnp.int32)
    slot_rank = jnp.sum((jnp.cumsum(flat_hot, axis=0) - flat_hot) * flat_hot, axis=1)
    rank_hot = slot_rank[:, None] == jnp.arange(capacity, dtype=jnp.int32)[None, :]
    placing = ((flat_hot[:, :, None] > 0) & rank_hot[:, None, :]).reshape(
        flat_hot.shape[0], expert_count * capacity
    )
    doubled = jnp.repeat(scaled, 2, axis=0)
    own_rows = jnp.einsum(
        "rs,rd->sd", placing.astype(jnp.bfloat16), doubled, preferred_element_type=jnp.float32
    ).astype(jnp.bfloat16)
    own_square = jnp.sum(jnp.where(placing, square[:, None], jnp.float32(0.0)), axis=0)
    own_lead = jnp.sum(jnp.where(placing, lead[:, None], jnp.float32(0.0)), axis=0)
    return own_rows, own_square, own_lead


def on_device(tokens, route, norm_gain, router, gate_weight, up_weight):
    expert_count, capacity = router.shape[1], 5 * route.shape[0] // 16
    half = capacity // 2
    slots = lax.axis_size("expert")
    start_local = lax.axis_index("section") * WIDTH
    as_float = tokens.astype(jnp.float32)
    square_part = jnp.sum(as_float * as_float, axis=-1)
    gain_local = lax.dynamic_slice_in_dim(norm_gain, start_local, WIDTH, 0)
    scaled = (as_float * gain_local).astype(jnp.bfloat16)
    router_local = lax.dynamic_slice_in_dim(router, start_local, WIDTH, 0)
    logit_part = jnp.dot(scaled, router_local, preferred_element_type=jnp.float32)
    own_rows, own_square, own_lead = place_rows(
        scaled, square_part, logit_part, route, expert_count, capacity
    )

    def to_slots(a, tail):
        a = a.reshape((expert_count, 1, 2) + tail)
        return jnp.broadcast_to(a, (expert_count, 2, 2) + tail).reshape((slots,) + tail)

    sent_rows = to_slots(own_rows, (half, WIDTH))
    sent_stat = jnp.stack(
        [to_slots(own_square, (half,)), to_slots(own_lead, (half,))], axis=1
    )
    recv_rows, recv_stat = (
        lax.all_to_all(sent_rows, "expert", split_axis=0, concat_axis=0, tiled=True),
        lax.all_to_all(sent_stat, "expert", split_axis=0, concat_axis=0, tiled=True),
    )
    stat = jnp.transpose(recv_stat, (1, 0, 2)).reshape(2, ROWS)
    stat = jnp.concatenate([stat, jnp.zeros((6, ROWS), jnp.float32)], axis=0)
    vmem = pl.BlockSpec(memory_space=pltpu.VMEM)
    acc, total = pl.pallas_call(
        gather_matmul,
        out_shape=(
            jax.ShapeDtypeStruct((2 * ROWS, 256), jnp.float32),
            jax.ShapeDtypeStruct((2, 8, ROWS), jnp.float32),
        ),
        in_specs=[vmem] * 4,
        out_specs=(vmem, vmem),
        scratch_shapes=[
            pltpu.VMEM((2 * Z, 2, ROWS, WIDTH), jnp.bfloat16),
            pltpu.VMEM((2 * Z, 2, 8, ROWS), jnp.float32),
            pltpu.SemaphoreType.DMA((COPIES,)),
            pltpu.SemaphoreType.DMA((COPIES,)),
            pltpu.SemaphoreType.DMA((2,)),
        ],
        compiler_params=pltpu.CompilerParams(
            collective_id=0, has_side_effects=True, vmem_limit_bytes=48 * 1024 * 1024
        ),
    )(recv_rows.reshape(ROWS, WIDTH), stat, gate_weight[0, 0], up_weight[0, 0])
    scale = lax.rsqrt(total[:, 0] / D + 1e-05)
    weight = (1.0 / (1.0 + jnp.exp(total[:, 1] * scale))).astype(jnp.bfloat16).astype(jnp.float32)
    acc = acc.reshape(2, slots, half, 256)
    scale = scale.reshape(2, slots, half, 1)
    weight = weight.reshape(2, slots, half, 1)
    result = jax.nn.silu(acc[..., :128] * scale) * (acc[..., 128:] * scale) * weight
    result = jnp.transpose(result.astype(jnp.bfloat16), (1, 0, 2, 3)).reshape(slots, capacity, 128)
    return result[None, :, :, None, :]


def solution(mesh):
    in_specs = (
        P("expert", "section"),
        P("expert", None),
        P(),
        P(),
        P("expert", "section", None, None),
        P("expert", "section", None, None),
    )
    out_specs = P("expert", None, None, "section", None)
    return jax.shard_map(
        on_device, mesh=mesh, in_specs=in_specs, out_specs=out_specs, check_vma=False
    )
```

```python
import jax
import jax.numpy as jnp
from jax import lax
from jax.experimental import pallas as pl
from jax.experimental.pallas import tpu as pltpu
from jax.sharding import PartitionSpec as P

D = 6144
Z = 8
ROWS = 640
WIDTH = 384
SPLIT = 208
MIDDLE = ROWS - 2 * SPLIT
COPIES = 86


def gather_matmul(own_ref, stat_ref, gate_ref, up_ref, acc_ref, tot_ref, full, stats, send, recv, local):
    sec = lax.axis_index("section")
    exp = lax.axis_index("expert")
    plane, z = sec // Z, lax.rem(sec, Z)
    core = lax.rem(exp, 2)
    odd = lax.rem(exp // 2, 2)
    up_sec = plane * Z + lax.rem(z + 1, Z)
    down_sec = plane * Z + lax.rem(z + Z - 1, Z)
    across_sec = (1 - plane) * Z + z
    peers = dict(
        up=(up_sec, exp),
        down=(down_sec, exp),
        across=(across_sec, exp),
        partner=(sec, exp + 1 - 2 * core),
        side=(sec, exp + 2 - 4 * odd),
    )
    barrier = pltpu.get_barrier_semaphore()
    for peer in peers.values():
        pl.semaphore_signal(barrier, inc=1, device_id=peer, device_id_type=pl.DeviceIdType.MESH)
    pl.semaphore_wait(barrier, len(peers))

    shift = (0, Z - 1, Z - 2, Z - 3, 1, 2, 3, 4)

    def mine(i):
        return plane * Z + lax.rem(z + shift[i], Z)

    def other(i):
        return (1 - plane) * Z + lax.rem(z + shift[i], Z)

    made = {}

    def start(name, peer, src, dst):
        n = len(made)
        copy = pltpu.make_async_remote_copy(
            src_ref=src,
            dst_ref=dst,
            send_sem=send.at[n],
            recv_sem=recv.at[n],
            device_id=peers[peer],
            device_id_type=pl.DeviceIdType.MESH,
        )
        copy.start()
        made[name] = copy

    def rows(i_sec, lo, n):
        return full.at[i_sec, core, pl.ds(pl.multiple_of(lo, 16), n)]

    def own_rows(lo, n):
        return own_ref.at[pl.ds(pl.multiple_of(lo, 16), n)]

    kept = (odd * (ROWS - SPLIT), SPLIT)
    rest = ((1 - odd) * SPLIT, ROWS - SPLIT)
    middle = (SPLIT, MIDDLE)

    def ring(kind, i, way, hop):
        lo, n = (odd * SPLIT, SPLIT + MIDDLE) if kind == 0 else kept
        if hop == 4:
            first = MIDDLE if kind == 0 else SPLIT // 2 + 8
            lo, n = (lo, first) if way == "up" else (lo + first, n - first)
        dst = rows(mine(i) if kind == 0 else other(i), lo, n)
        start(("ring", kind, way, hop), way, own_rows(lo, n) if kind == 0 and i == 0 else dst, dst)

    def ring_stat(i, way, hop):
        dst = stats.at[mine(i), core]
        start(("stat", way, hop), way, stat_ref if i == 0 else dst, dst)

    def spread(i):
        if i:
            dst = rows(mine(i), *middle)
            start(("late", i), "across", dst, dst)
            dst = rows(mine(i), *kept)
            start(("y0", i), "side", dst, dst)
        dst = stats.at[mine(i), core]
        src = stat_ref if i == 0 else dst
        start(("sx", i), "across", src, dst)
        start(("ps", i), "partner", src, dst)

    def spread_other(i):
        dst = rows(other(i), *kept)
        start(("y1", i), "side", dst, dst)

    def whole(i):
        if i:
            made[("y0", i)].wait_recv()
            dst = rows(mine(i), 0, ROWS)
            start(("p0", i), "partner", dst, dst)
            made[("late", i)].wait_recv()
            made[("y1", i)].wait_recv()
        else:
            made[("rest",)].wait_recv()
        dst = rows(other(i), 0, ROWS)
        start(("p1", i), "partner", dst, dst)
        made[("sx", i)].wait_recv()
        dst = stats.at[other(i), core]
        start(("po", i), "partner", dst, dst)

    def multiply(s, first):
        cols = pl.ds(pl.multiple_of(s * WIDTH, 128), WIDTH)
        weights = jnp.concatenate([gate_ref[:, cols], up_ref[:, cols]], axis=0)

        @pl.loop(0, 4)
        def _(t):
            at = pl.ds(pl.multiple_of(lax.rem(t, 2) * 320, 32), 320)
            to = pl.ds(pl.multiple_of(t * 320, 32), 320)
            part = lax.dot_general(
                full[s, t // 2, at, :], weights, (((1,), (1,)), ((), ())),
                preferred_element_type=jnp.float32,
            )
            if first:
                acc_ref[to, :] = part
            else:
                acc_ref[to, :] += part

    def consume(i):
        made[("p0", i)].wait_recv()
        multiply(mine(i), i == 0)
        made[("p1", i)].wait_recv()
        multiply(other(i), False)

    start(("kept",), "across", own_rows(*kept), rows(sec, *kept))
    ring(0, 0, "up", 1)
    ring(0, 0, "down", 1)
    ring_stat(0, "up", 1)
    ring_stat(0, "down", 1)
    start(("rest",), "across", own_rows(*rest), rows(sec, *rest))
    start(("p0", 0), "partner", own_ref, rows(sec, 0, ROWS))
    spread(0)
    keep = pltpu.make_async_copy(own_ref, full.at[sec, core], local.at[0])
    keep.start()
    keep_stat = pltpu.make_async_copy(stat_ref, stats.at[sec, core], local.at[1])
    keep_stat.start()
    made[("kept",)].wait_recv()
    ring(1, 0, "up", 1)
    ring(1, 0, "down", 1)
    keep.wait()
    keep_stat.wait()
    ways = (("up", 0), ("down", 3))
    for hop in (1, 2, 3):
        for way, base in ways:
            made[("ring", 0, way, hop)].wait_recv()
            ring(0, base + hop, way, hop + 1)
            made[("stat", way, hop)].wait_recv()
            if hop < 3 or way == "up":
                ring_stat(base + hop, way, hop + 1)
            spread(base + hop)
        for way, base in ways:
            made[("ring", 1, way, hop)].wait_recv()
            ring(1, base + hop, way, hop + 1)
            spread_other(base + hop)
        before = [0] if hop == 1 else [hop - 1, hop + 2]
        for i in before:
            whole(i)
        for i in before:
            consume(i)
    for way, _ in ways:
        made[("ring", 0, way, 4)].wait_recv()
    made[("stat", "up", 4)].wait_recv()
    spread(7)
    for way, _ in ways:
        made[("ring", 1, way, 4)].wait_recv()
    spread_other(7)
    for i in (3, 6):
        whole(i)
    for i in (3, 6):
        consume(i)
    whole(7)
    consume(7)
    for i in range(8):
        made[("ps", i)].wait_recv()
        made[("po", i)].wait_recv()
    tot_ref[...] = jnp.sum(stats[...], axis=0)
    for copy in made.values():
        copy.wait_send()


def place_rows(scaled, square_part, logit_part, route, expert_count, capacity):
    one_hot = route[:, :, None] == jnp.arange(expert_count, dtype=jnp.int32)[None, None, :]
    picked = jnp.sum(jnp.where(one_hot, logit_part[:, None, :], jnp.float32(0.0)), axis=-1)
    lead = jnp.stack([picked[:, 1] - picked[:, 0], picked[:, 0] - picked[:, 1]], axis=1).reshape(-1)
    square = jnp.repeat(square_part, 2)
    flat_hot = one_hot.reshape(-1, expert_count).astype(jnp.int32)
    slot_rank = jnp.sum((jnp.cumsum(flat_hot, axis=0) - flat_hot) * flat_hot, axis=1)
    rank_hot = slot_rank[:, None] == jnp.arange(capacity, dtype=jnp.int32)[None, :]
    placing = ((flat_hot[:, :, None] > 0) & rank_hot[:, None, :]).reshape(
        flat_hot.shape[0], expert_count * capacity
    )
    doubled = jnp.repeat(scaled, 2, axis=0)
    own_rows = jnp.einsum(
        "rs,rd->sd", placing.astype(jnp.bfloat16), doubled, preferred_element_type=jnp.float32
    ).astype(jnp.bfloat16)
    own_square = jnp.sum(jnp.where(placing, square[:, None], jnp.float32(0.0)), axis=0)
    own_lead = jnp.sum(jnp.where(placing, lead[:, None], jnp.float32(0.0)), axis=0)
    return own_rows, own_square, own_lead


def on_device(tokens, route, norm_gain, router, gate_weight, up_weight):
    expert_count, capacity = router.shape[1], 5 * route.shape[0] // 16
    half = capacity // 2
    slots = lax.axis_size("expert")
    start_local = lax.axis_index("section") * WIDTH
    as_float = tokens.astype(jnp.float32)
    square_part = jnp.sum(as_float * as_float, axis=-1)
    gain_local = lax.dynamic_slice_in_dim(norm_gain, start_local, WIDTH, 0)
    scaled = (as_float * gain_local).astype(jnp.bfloat16)
    router_local = lax.dynamic_slice_in_dim(router, start_local, WIDTH, 0)
    logit_part = jnp.dot(scaled, router_local, preferred_element_type=jnp.float32)
    own_rows, own_square, own_lead = place_rows(
        scaled, square_part, logit_part, route, expert_count, capacity
    )

    def to_slots(a, tail):
        a = a.reshape((expert_count, 1, 2) + tail)
        return jnp.broadcast_to(a, (expert_count, 2, 2) + tail).reshape((slots,) + tail)

    def thirds(v):
        high = lax.reduce_precision(v, 8, 7)
        middle = lax.reduce_precision(v - high, 8, 7)
        return [high, middle, v - high - middle]

    parts = jnp.stack(thirds(own_square) + thirds(own_lead)).astype(jnp.bfloat16)
    parts = jnp.transpose(parts.reshape(6, 2 * expert_count, half), (1, 0, 2))
    parts = parts.reshape(2 * expert_count, 1, 6 * half)
    parts = jnp.pad(parts, ((0, 0), (0, 0), (0, WIDTH - 6 * half)))
    block = jnp.concatenate([own_rows.reshape(2 * expert_count, half, WIDTH), parts], axis=1)
    sent = to_slots(block, (half + 1, WIDTH))
    received = lax.all_to_all(sent, "expert", split_axis=0, concat_axis=0, tiled=True)
    recv_rows = received[:, :half]
    stat = received[:, half, : 6 * half].astype(jnp.float32).reshape(slots, 2, 3, half)
    stat = jnp.transpose(stat[:, :, 0] + stat[:, :, 1] + stat[:, :, 2], (1, 0, 2)).reshape(2, ROWS)
    stat = jnp.concatenate([stat, jnp.zeros((6, ROWS), jnp.float32)], axis=0)
    vmem = pl.BlockSpec(memory_space=pltpu.VMEM)
    acc, total = pl.pallas_call(
        gather_matmul,
        out_shape=(
            jax.ShapeDtypeStruct((2 * ROWS, 256), jnp.float32),
            jax.ShapeDtypeStruct((2, 8, ROWS), jnp.float32),
        ),
        in_specs=[vmem] * 4,
        out_specs=(vmem, vmem),
        scratch_shapes=[
            pltpu.VMEM((2 * Z, 2, ROWS, WIDTH), jnp.bfloat16),
            pltpu.VMEM((2 * Z, 2, 8, ROWS), jnp.float32),
            pltpu.SemaphoreType.DMA((COPIES,)),
            pltpu.SemaphoreType.DMA((COPIES,)),
            pltpu.SemaphoreType.DMA((2,)),
        ],
        compiler_params=pltpu.CompilerParams(
            collective_id=0, has_side_effects=True, vmem_limit_bytes=48 * 1024 * 1024
        ),
    )(recv_rows.reshape(ROWS, WIDTH), stat, gate_weight[0, 0], up_weight[0, 0])
    scale = lax.rsqrt(total[:, 0] / D + 1e-05)
    weight = (1.0 / (1.0 + jnp.exp(total[:, 1] * scale))).astype(jnp.bfloat16).astype(jnp.float32)
    acc = acc.reshape(2, slots, half, 256)
    scale = scale.reshape(2, slots, half, 1)
    weight = weight.reshape(2, slots, half, 1)
    result = jax.nn.silu(acc[..., :128] * scale) * (acc[..., 128:] * scale) * weight
    result = jnp.transpose(result.astype(jnp.bfloat16), (1, 0, 2, 3)).reshape(slots, capacity, 128)
    return result[None, :, :, None, :]


def solution(mesh):
    in_specs = (
        P("expert", "section"),
        P("expert", None),
        P(),
        P(),
        P("expert", "section", None, None),
        P("expert", "section", None, None),
    )
    out_specs = P("expert", None, None, "section", None)
    return jax.shard_map(
        on_device, mesh=mesh, in_specs=in_specs, out_specs=out_specs, check_vma=False
    )
```

```python
import jax
import jax.numpy as jnp
from jax import lax
from jax.experimental import pallas as pl
from jax.experimental.pallas import tpu as pltpu
from jax.sharding import PartitionSpec as P

D = 6144
Z = 8
ROWS = 640
WIDTH = 384
SPLIT = 192
AHEAD = 144
LATE = ROWS - 2 * SPLIT - AHEAD
COPIES = 96


def gather_matmul(own_ref, stat_ref, gate_ref, up_ref, acc_ref, tot_ref, full, stats, send, recv, local):
    sec = lax.axis_index("section")
    exp = lax.axis_index("expert")
    plane, z = sec // Z, lax.rem(sec, Z)
    core = lax.rem(exp, 2)
    odd = lax.rem(exp // 2, 2)
    up_sec = plane * Z + lax.rem(z + 1, Z)
    down_sec = plane * Z + lax.rem(z + Z - 1, Z)
    across_sec = (1 - plane) * Z + z
    peers = dict(
        up=(up_sec, exp),
        down=(down_sec, exp),
        across=(across_sec, exp),
        partner=(sec, exp + 1 - 2 * core),
        side=(sec, exp + 2 - 4 * odd),
    )
    barrier = pltpu.get_barrier_semaphore()
    for peer in peers.values():
        pl.semaphore_signal(barrier, inc=1, device_id=peer, device_id_type=pl.DeviceIdType.MESH)
    pl.semaphore_wait(barrier, len(peers))

    shift = (0, Z - 1, Z - 2, Z - 3, 1, 2, 3, 4)

    def mine(i):
        return plane * Z + lax.rem(z + shift[i], Z)

    def other(i):
        return (1 - plane) * Z + lax.rem(z + shift[i], Z)

    made = {}

    def start(name, peer, src, dst):
        n = len(made)
        copy = pltpu.make_async_remote_copy(
            src_ref=src,
            dst_ref=dst,
            send_sem=send.at[n],
            recv_sem=recv.at[n],
            device_id=peers[peer],
            device_id_type=pl.DeviceIdType.MESH,
        )
        copy.start()
        made[name] = copy

    def rows(i_sec, lo, n):
        return full.at[i_sec, core, pl.ds(pl.multiple_of(lo, 16), n)]

    def own_rows(lo, n):
        return own_ref.at[pl.ds(pl.multiple_of(lo, 16), n)]

    kept = (odd * (ROWS - SPLIT), SPLIT)
    ahead = (SPLIT, AHEAD)
    late = (SPLIT + AHEAD, LATE)

    def ring(kind, i, way, hop):
        lo, n = ((odd * SPLIT, ROWS - SPLIT), kept, ahead)[kind]
        if hop == 4:
            first = (n + 31) // 32 * 16
            lo, n = (lo, first) if way == "up" else (lo + first, n - first)
        dst = rows(mine(i) if kind == 0 else other(i), lo, n)
        start(("ring", kind, way, hop), way, own_rows(lo, n) if kind == 0 and i == 0 else dst, dst)

    def ring_stat(i, way, hop):
        dst = stats.at[mine(i), core]
        start(("stat", way, hop), way, stat_ref if i == 0 else dst, dst)

    def spread(i):
        if i:
            dst = rows(mine(i), *late)
            start(("late", i), "across", dst, dst)
            dst = rows(mine(i), *kept)
            start(("y0", i), "side", dst, dst)
        dst = stats.at[mine(i), core]
        src = stat_ref if i == 0 else dst
        start(("sx", i), "across", src, dst)
        start(("ps", i), "partner", src, dst)

    def spread_other(i):
        dst = rows(other(i), *kept)
        start(("y1", i), "side", dst, dst)

    def whole(i):
        if i:
            made[("y0", i)].wait_recv()
            dst = rows(mine(i), 0, ROWS)
            start(("p0", i), "partner", dst, dst)
            made[("late", i)].wait_recv()
        else:
            made[("late own",)].wait_recv()
        made[("y1", i)].wait_recv()
        dst = rows(other(i), 0, ROWS)
        start(("p1", i), "partner", dst, dst)
        made[("sx", i)].wait_recv()
        dst = stats.at[other(i), core]
        start(("po", i), "partner", dst, dst)

    def multiply(s, first):
        cols = pl.ds(pl.multiple_of(s * WIDTH, 128), WIDTH)
        weights = jnp.concatenate([gate_ref[:, cols], up_ref[:, cols]], axis=0)

        @pl.loop(0, 4)
        def _(t):
            at = pl.ds(pl.multiple_of(lax.rem(t, 2) * 320, 32), 320)
            to = pl.ds(pl.multiple_of(t * 320, 32), 320)
            part = lax.dot_general(
                full[s, t // 2, at, :], weights, (((1,), (1,)), ((), ())),
                preferred_element_type=jnp.float32,
            )
            if first:
                acc_ref[to, :] = part
            else:
                acc_ref[to, :] += part

    def consume(i):
        made[("p0", i)].wait_recv()
        multiply(mine(i), i == 0)
        made[("p1", i)].wait_recv()
        multiply(other(i), False)

    start(("kept",), "across", own_rows(*kept), rows(sec, *kept))
    ring(0, 0, "up", 1)
    ring(0, 0, "down", 1)
    ring_stat(0, "up", 1)
    ring_stat(0, "down", 1)
    start(("ahead",), "across", own_rows(*ahead), rows(sec, *ahead))
    start(("late own",), "across", own_rows(*late), rows(sec, *late))
    start(("p0", 0), "partner", own_ref, rows(sec, 0, ROWS))
    spread(0)
    keep = pltpu.make_async_copy(own_ref, full.at[sec, core], local.at[0])
    keep.start()
    keep_stat = pltpu.make_async_copy(stat_ref, stats.at[sec, core], local.at[1])
    keep_stat.start()
    made[("kept",)].wait_recv()
    ring(1, 0, "up", 1)
    ring(1, 0, "down", 1)
    spread_other(0)
    made[("ahead",)].wait_recv()
    ring(2, 0, "up", 1)
    ring(2, 0, "down", 1)
    keep.wait()
    keep_stat.wait()
    ways = (("up", 0), ("down", 3))
    for hop in (1, 2, 3):
        for way, base in ways:
            made[("ring", 0, way, hop)].wait_recv()
            ring(0, base + hop, way, hop + 1)
            made[("stat", way, hop)].wait_recv()
            if hop < 3 or way == "up":
                ring_stat(base + hop, way, hop + 1)
            spread(base + hop)
        for way, base in ways:
            made[("ring", 1, way, hop)].wait_recv()
            ring(1, base + hop, way, hop + 1)
            spread_other(base + hop)
        for way, base in ways:
            made[("ring", 2, way, hop)].wait_recv()
            ring(2, base + hop, way, hop + 1)
        before = [0] if hop == 1 else [hop - 1, hop + 2]
        for i in before:
            whole(i)
        for i in before:
            consume(i)
    for way, _ in ways:
        made[("ring", 0, way, 4)].wait_recv()
    made[("stat", "up", 4)].wait_recv()
    spread(7)
    for way, _ in ways:
        made[("ring", 1, way, 4)].wait_recv()
    spread_other(7)
    for way, _ in ways:
        made[("ring", 2, way, 4)].wait_recv()
    for i in (3, 6):
        whole(i)
    for i in (3, 6):
        consume(i)
    whole(7)
    consume(7)
    for i in range(8):
        made[("ps", i)].wait_recv()
        made[("po", i)].wait_recv()
    tot_ref[...] = jnp.sum(stats[...], axis=0)
    for copy in made.values():
        copy.wait_send()


def place_rows(scaled, square_part, logit_part, route, expert_count, capacity):
    one_hot = route[:, :, None] == jnp.arange(expert_count, dtype=jnp.int32)[None, None, :]
    picked = jnp.sum(jnp.where(one_hot, logit_part[:, None, :], jnp.float32(0.0)), axis=-1)
    lead = jnp.stack([picked[:, 1] - picked[:, 0], picked[:, 0] - picked[:, 1]], axis=1).reshape(-1)
    square = jnp.repeat(square_part, 2)
    flat_hot = one_hot.reshape(-1, expert_count).astype(jnp.int32)
    slot_rank = jnp.sum((jnp.cumsum(flat_hot, axis=0) - flat_hot) * flat_hot, axis=1)
    rank_hot = slot_rank[:, None] == jnp.arange(capacity, dtype=jnp.int32)[None, :]
    placing = ((flat_hot[:, :, None] > 0) & rank_hot[:, None, :]).reshape(
        flat_hot.shape[0], expert_count * capacity
    )
    doubled = jnp.repeat(scaled, 2, axis=0)
    own_rows = jnp.einsum(
        "rs,rd->sd", placing.astype(jnp.bfloat16), doubled, preferred_element_type=jnp.float32
    ).astype(jnp.bfloat16)
    own_square = jnp.sum(jnp.where(placing, square[:, None], jnp.float32(0.0)), axis=0)
    own_lead = jnp.sum(jnp.where(placing, lead[:, None], jnp.float32(0.0)), axis=0)
    return own_rows, own_square, own_lead


def on_device(tokens, route, norm_gain, router, gate_weight, up_weight):
    expert_count, capacity = router.shape[1], 5 * route.shape[0] // 16
    half = capacity // 2
    slots = lax.axis_size("expert")
    start_local = lax.axis_index("section") * WIDTH
    as_float = tokens.astype(jnp.float32)
    square_part = jnp.sum(as_float * as_float, axis=-1)
    gain_local = lax.dynamic_slice_in_dim(norm_gain, start_local, WIDTH, 0)
    scaled = (as_float * gain_local).astype(jnp.bfloat16)
    router_local = lax.dynamic_slice_in_dim(router, start_local, WIDTH, 0)
    logit_part = jnp.dot(scaled, router_local, preferred_element_type=jnp.float32)
    own_rows, own_square, own_lead = place_rows(
        scaled, square_part, logit_part, route, expert_count, capacity
    )

    def to_slots(a, tail):
        a = a.reshape((expert_count, 1, 2) + tail)
        return jnp.broadcast_to(a, (expert_count, 2, 2) + tail).reshape((slots,) + tail)

    def thirds(v):
        high = lax.reduce_precision(v, 8, 7)
        middle = lax.reduce_precision(v - high, 8, 7)
        return [high, middle, v - high - middle]

    parts = jnp.stack(thirds(own_square) + thirds(own_lead)).astype(jnp.bfloat16)
    parts = jnp.transpose(parts.reshape(6, 2 * expert_count, half), (1, 0, 2))
    parts = parts.reshape(2 * expert_count, 1, 6 * half)
    parts = jnp.pad(parts, ((0, 0), (0, 0), (0, WIDTH - 6 * half)))
    block = jnp.concatenate([own_rows.reshape(2 * expert_count, half, WIDTH), parts], axis=1)
    sent = to_slots(block, (half + 1, WIDTH))
    received = lax.all_to_all(sent, "expert", split_axis=0, concat_axis=0, tiled=True)
    recv_rows = received[:, :half]
    stat = received[:, half, : 6 * half].astype(jnp.float32).reshape(slots, 2, 3, half)
    stat = jnp.transpose(stat[:, :, 0] + stat[:, :, 1] + stat[:, :, 2], (1, 0, 2)).reshape(2, ROWS)
    stat = jnp.concatenate([stat, jnp.zeros((6, ROWS), jnp.float32)], axis=0)
    vmem = pl.BlockSpec(memory_space=pltpu.VMEM)
    acc, total = pl.pallas_call(
        gather_matmul,
        out_shape=(
            jax.ShapeDtypeStruct((2 * ROWS, 256), jnp.float32),
            jax.ShapeDtypeStruct((2, 8, ROWS), jnp.float32),
        ),
        in_specs=[vmem] * 4,
        out_specs=(vmem, vmem),
        scratch_shapes=[
            pltpu.VMEM((2 * Z, 2, ROWS, WIDTH), jnp.bfloat16),
            pltpu.VMEM((2 * Z, 2, 8, ROWS), jnp.float32),
            pltpu.SemaphoreType.DMA((COPIES,)),
            pltpu.SemaphoreType.DMA((COPIES,)),
            pltpu.SemaphoreType.DMA((2,)),
        ],
        compiler_params=pltpu.CompilerParams(
            collective_id=0, has_side_effects=True, vmem_limit_bytes=48 * 1024 * 1024
        ),
    )(recv_rows.reshape(ROWS, WIDTH), stat, gate_weight[0, 0], up_weight[0, 0])
    scale = lax.rsqrt(total[:, 0] / D + 1e-05)
    weight = (1.0 / (1.0 + jnp.exp(total[:, 1] * scale))).astype(jnp.bfloat16).astype(jnp.float32)
    acc = acc.reshape(2, slots, half, 256)
    scale = scale.reshape(2, slots, half, 1)
    weight = weight.reshape(2, slots, half, 1)
    result = jax.nn.silu(acc[..., :128] * scale) * (acc[..., 128:] * scale) * weight
    result = jnp.transpose(result.astype(jnp.bfloat16), (1, 0, 2, 3)).reshape(slots, capacity, 128)
    return result[None, :, :, None, :]


def solution(mesh):
    in_specs = (
        P("expert", "section"),
        P("expert", None),
        P(),
        P(),
        P("expert", "section", None, None),
        P("expert", "section", None, None),
    )
    out_specs = P("expert", None, None, "section", None)
    return jax.shard_map(
        on_device, mesh=mesh, in_specs=in_specs, out_specs=out_specs, check_vma=False
    )
```

```python
import jax
import jax.numpy as jnp
from jax import lax
from jax.experimental import pallas as pl
from jax.experimental.pallas import tpu as pltpu
from jax.sharding import PartitionSpec as P

D = 6144
Z = 8
ROWS = 640
WIDTH = 384
SPLIT = 192
AHEAD = 144
LATE = ROWS - 2 * SPLIT - AHEAD
COPIES = 96


def gather_matmul(own_ref, stat_ref, gate_ref, up_ref, acc_ref, tot_ref, full, stats, send, recv, local):
    sec = lax.axis_index("section")
    exp = lax.axis_index("expert")
    plane, z = sec // Z, lax.rem(sec, Z)
    core = lax.rem(exp, 2)
    odd = lax.rem(exp // 2, 2)
    up_sec = plane * Z + lax.rem(z + 1, Z)
    down_sec = plane * Z + lax.rem(z + Z - 1, Z)
    across_sec = (1 - plane) * Z + z
    peers = dict(
        up=(up_sec, exp),
        down=(down_sec, exp),
        across=(across_sec, exp),
        partner=(sec, exp + 1 - 2 * core),
        side=(sec, exp + 2 - 4 * odd),
    )
    barrier = pltpu.get_barrier_semaphore()
    for peer in peers.values():
        pl.semaphore_signal(barrier, inc=1, device_id=peer, device_id_type=pl.DeviceIdType.MESH)
    pl.semaphore_wait(barrier, len(peers))

    shift = (0, Z - 1, Z - 2, Z - 3, 1, 2, 3, 4)

    def mine(i):
        return plane * Z + lax.rem(z + shift[i], Z)

    def other(i):
        return (1 - plane) * Z + lax.rem(z + shift[i], Z)

    made = {}

    def start(name, peer, src, dst):
        n = len(made)
        copy = pltpu.make_async_remote_copy(
            src_ref=src,
            dst_ref=dst,
            send_sem=send.at[n],
            recv_sem=recv.at[n],
            device_id=peers[peer],
            device_id_type=pl.DeviceIdType.MESH,
        )
        copy.start()
        made[name] = copy

    def rows(i_sec, lo, n):
        return full.at[i_sec, core, pl.ds(pl.multiple_of(lo, 16), n)]

    def own_rows(lo, n):
        return own_ref.at[pl.ds(pl.multiple_of(lo, 16), n)]

    kept = (odd * (ROWS - SPLIT), SPLIT)
    ahead = (SPLIT, AHEAD)
    late = (SPLIT + AHEAD, LATE)

    def ring(kind, i, way, hop):
        lo, n = ((odd * SPLIT, ROWS - SPLIT), kept, ahead)[kind]
        if hop == 4:
            first = (n + 31) // 32 * 16
            lo, n = (lo, first) if way == "up" else (lo + first, n - first)
        dst = rows(mine(i) if kind == 0 else other(i), lo, n)
        start(("ring", kind, way, hop), way, own_rows(lo, n) if kind == 0 and i == 0 else dst, dst)

    def ring_stat(i, way, hop):
        dst = stats.at[mine(i), core]
        start(("stat", way, hop), way, stat_ref if i == 0 else dst, dst)

    def spread(i):
        if i:
            dst = rows(mine(i), *late)
            start(("late", i), "across", dst, dst)
            dst = rows(mine(i), *kept)
            start(("y0", i), "side", dst, dst)
        dst = stats.at[mine(i), core]
        src = stat_ref if i == 0 else dst
        start(("sx", i), "across", src, dst)
        start(("ps", i), "partner", src, dst)

    def spread_other(i):
        dst = rows(other(i), *kept)
        start(("y1", i), "side", dst, dst)

    def whole(i):
        if i:
            made[("y0", i)].wait_recv()
            dst = rows(mine(i), 0, ROWS)
            start(("p0", i), "partner", dst, dst)
            made[("late", i)].wait_recv()
        else:
            made[("late own",)].wait_recv()
        made[("y1", i)].wait_recv()
        dst = rows(other(i), 0, ROWS)
        start(("p1", i), "partner", dst, dst)
        made[("sx", i)].wait_recv()
        dst = stats.at[other(i), core]
        start(("po", i), "partner", dst, dst)

    def multiply(s, first):
        cols = pl.ds(pl.multiple_of(s * WIDTH, 128), WIDTH)
        weights = jnp.concatenate([gate_ref[:, cols], up_ref[:, cols]], axis=0)

        @pl.loop(0, 2)
        def _(t):
            to = pl.ds(pl.multiple_of(t * ROWS, 128), ROWS)
            part = lax.dot_general(
                full[s, t], weights, (((1,), (1,)), ((), ())),
                preferred_element_type=jnp.float32,
            )
            if first:
                acc_ref[to, :] = part
            else:
                acc_ref[to, :] += part

    def consume(i):
        made[("p0", i)].wait_recv()
        multiply(mine(i), i == 0)
        made[("p1", i)].wait_recv()
        multiply(other(i), False)

    start(("kept",), "across", own_rows(*kept), rows(sec, *kept))
    ring(0, 0, "up", 1)
    ring(0, 0, "down", 1)
    ring_stat(0, "up", 1)
    ring_stat(0, "down", 1)
    start(("ahead",), "across", own_rows(*ahead), rows(sec, *ahead))
    start(("late own",), "across", own_rows(*late), rows(sec, *late))
    start(("p0", 0), "partner", own_ref, rows(sec, 0, ROWS))
    spread(0)
    keep = pltpu.make_async_copy(own_ref, full.at[sec, core], local.at[0])
    keep.start()
    keep_stat = pltpu.make_async_copy(stat_ref, stats.at[sec, core], local.at[1])
    keep_stat.start()
    made[("kept",)].wait_recv()
    ring(1, 0, "up", 1)
    ring(1, 0, "down", 1)
    spread_other(0)
    made[("ahead",)].wait_recv()
    ring(2, 0, "up", 1)
    ring(2, 0, "down", 1)
    keep.wait()
    keep_stat.wait()
    ways = (("up", 0), ("down", 3))
    for hop in (1, 2, 3):
        for way, base in ways:
            made[("ring", 0, way, hop)].wait_recv()
            ring(0, base + hop, way, hop + 1)
            made[("stat", way, hop)].wait_recv()
            if hop < 3 or way == "up":
                ring_stat(base + hop, way, hop + 1)
            spread(base + hop)
        for way, base in ways:
            made[("ring", 1, way, hop)].wait_recv()
            ring(1, base + hop, way, hop + 1)
            spread_other(base + hop)
        for way, base in ways:
            made[("ring", 2, way, hop)].wait_recv()
            ring(2, base + hop, way, hop + 1)
        before = [0] if hop == 1 else [hop - 1, hop + 2]
        for i in before:
            whole(i)
        for i in before:
            consume(i)
    for way, _ in ways:
        made[("ring", 0, way, 4)].wait_recv()
    made[("stat", "up", 4)].wait_recv()
    spread(7)
    for way, _ in ways:
        made[("ring", 1, way, 4)].wait_recv()
    spread_other(7)
    for way, _ in ways:
        made[("ring", 2, way, 4)].wait_recv()
    for i in (3, 6):
        whole(i)
    for i in (3, 6):
        consume(i)
    whole(7)
    consume(7)
    for i in range(8):
        made[("ps", i)].wait_recv()
        made[("po", i)].wait_recv()
    tot_ref[...] = jnp.sum(stats[...], axis=0)
    for copy in made.values():
        copy.wait_send()


def place_rows(scaled, square_part, logit_part, route, expert_count, capacity):
    one_hot = route[:, :, None] == jnp.arange(expert_count, dtype=jnp.int32)[None, None, :]
    picked = jnp.sum(jnp.where(one_hot, logit_part[:, None, :], jnp.float32(0.0)), axis=-1)
    lead = jnp.stack([picked[:, 1] - picked[:, 0], picked[:, 0] - picked[:, 1]], axis=1).reshape(-1)
    square = jnp.repeat(square_part, 2)
    flat_hot = one_hot.reshape(-1, expert_count).astype(jnp.int32)
    slot_rank = jnp.sum((jnp.cumsum(flat_hot, axis=0) - flat_hot) * flat_hot, axis=1)
    rank_hot = slot_rank[:, None] == jnp.arange(capacity, dtype=jnp.int32)[None, :]
    placing = ((flat_hot[:, :, None] > 0) & rank_hot[:, None, :]).reshape(
        flat_hot.shape[0], expert_count * capacity
    )
    doubled = jnp.repeat(scaled, 2, axis=0)
    own_rows = jnp.einsum(
        "rs,rd->sd", placing.astype(jnp.bfloat16), doubled, preferred_element_type=jnp.float32
    ).astype(jnp.bfloat16)
    own_square = jnp.sum(jnp.where(placing, square[:, None], jnp.float32(0.0)), axis=0)
    own_lead = jnp.sum(jnp.where(placing, lead[:, None], jnp.float32(0.0)), axis=0)
    return own_rows, own_square, own_lead


def on_device(tokens, route, norm_gain, router, gate_weight, up_weight):
    expert_count, capacity = router.shape[1], 5 * route.shape[0] // 16
    half = capacity // 2
    slots = lax.axis_size("expert")
    start_local = lax.axis_index("section") * WIDTH
    as_float = tokens.astype(jnp.float32)
    square_part = jnp.sum(as_float * as_float, axis=-1)
    gain_local = lax.dynamic_slice_in_dim(norm_gain, start_local, WIDTH, 0)
    scaled = (as_float * gain_local).astype(jnp.bfloat16)
    router_local = lax.dynamic_slice_in_dim(router, start_local, WIDTH, 0)
    logit_part = jnp.dot(scaled, router_local, preferred_element_type=jnp.float32)
    own_rows, own_square, own_lead = place_rows(
        scaled, square_part, logit_part, route, expert_count, capacity
    )

    def to_slots(a, tail):
        a = a.reshape((expert_count, 1, 2) + tail)
        return jnp.broadcast_to(a, (expert_count, 2, 2) + tail).reshape((slots,) + tail)

    def thirds(v):
        high = lax.reduce_precision(v, 8, 7)
        middle = lax.reduce_precision(v - high, 8, 7)
        return [high, middle, v - high - middle]

    parts = jnp.stack(thirds(own_square) + thirds(own_lead)).astype(jnp.bfloat16)
    parts = jnp.transpose(parts.reshape(6, 2 * expert_count, half), (1, 0, 2))
    parts = parts.reshape(2 * expert_count, 1, 6 * half)
    parts = jnp.pad(parts, ((0, 0), (0, 0), (0, WIDTH - 6 * half)))
    block = jnp.concatenate([own_rows.reshape(2 * expert_count, half, WIDTH), parts], axis=1)
    sent = to_slots(block, (half + 1, WIDTH))
    received = lax.all_to_all(sent, "expert", split_axis=0, concat_axis=0, tiled=True)
    recv_rows = received[:, :half]
    stat = received[:, half, : 6 * half].astype(jnp.float32).reshape(slots, 2, 3, half)
    stat = jnp.transpose(stat[:, :, 0] + stat[:, :, 1] + stat[:, :, 2], (1, 0, 2)).reshape(2, ROWS)
    stat = jnp.concatenate([stat, jnp.zeros((6, ROWS), jnp.float32)], axis=0)
    vmem = pl.BlockSpec(memory_space=pltpu.VMEM)
    acc, total = pl.pallas_call(
        gather_matmul,
        out_shape=(
            jax.ShapeDtypeStruct((2 * ROWS, 256), jnp.float32),
            jax.ShapeDtypeStruct((2, 8, ROWS), jnp.float32),
        ),
        in_specs=[vmem] * 4,
        out_specs=(vmem, vmem),
        scratch_shapes=[
            pltpu.VMEM((2 * Z, 2, ROWS, WIDTH), jnp.bfloat16),
            pltpu.VMEM((2 * Z, 2, 8, ROWS), jnp.float32),
            pltpu.SemaphoreType.DMA((COPIES,)),
            pltpu.SemaphoreType.DMA((COPIES,)),
            pltpu.SemaphoreType.DMA((2,)),
        ],
        compiler_params=pltpu.CompilerParams(
            collective_id=0, has_side_effects=True, vmem_limit_bytes=48 * 1024 * 1024
        ),
    )(recv_rows.reshape(ROWS, WIDTH), stat, gate_weight[0, 0], up_weight[0, 0])
    scale = lax.rsqrt(total[:, 0] / D + 1e-05)
    weight = (1.0 / (1.0 + jnp.exp(total[:, 1] * scale))).astype(jnp.bfloat16).astype(jnp.float32)
    acc = acc.reshape(2, slots, half, 256)
    scale = scale.reshape(2, slots, half, 1)
    weight = weight.reshape(2, slots, half, 1)
    result = jax.nn.silu(acc[..., :128] * scale) * (acc[..., 128:] * scale) * weight
    result = jnp.transpose(result.astype(jnp.bfloat16), (1, 0, 2, 3)).reshape(slots, capacity, 128)
    return result[None, :, :, None, :]


def solution(mesh):
    in_specs = (
        P("expert", "section"),
        P("expert", None),
        P(),
        P(),
        P("expert", "section", None, None),
        P("expert", "section", None, None),
    )
    out_specs = P("expert", None, None, "section", None)
    return jax.shard_map(
        on_device, mesh=mesh, in_specs=in_specs, out_specs=out_specs, check_vma=False
    )
```
